32 devices in a mesh: sec: 8 (over z, core), op: 4 (over y, x).
Axes of the slice: x: 2, y: 2, z: 4, core: 2. Of those that a mesh axis runs over, the one named last changes fastest.
Arguments:
- theta: float32 [16, 512, 512], P('sec', 'op'), may hold values from -6 to 6
- counts: int32 [16], P('sec'), may hold values from 256 to 512, as said below
- pair_source: int32 [32], P('sec'), may hold values from 0 to 1
- pair_target: int32 [32], P('sec'), may hold values from 0 to 15
- left_ops: float32 [128, 512, 512], P(('sec', 'op')), may hold values from -0.25 to 0.25
- right_ops: float32 [128, 512, 512], P(('sec', 'op')), may hold values from -0.25 to 0.25
Outputs:
- cheb_last: float32 [16, 512, 512], P('sec', 'op')
- cheb_prev: float32 [16, 512, 512], P('sec', 'op')
The draws below stay inside these ranges and needn't reach their ends.
Inputs may be any that keep to these rules, and one draw needn't show every extreme that they name: `counts`: every sector has between 256 and 512 live states; some sector has exactly 512 and some exactly 256.
All inputs are finite; a program needn't handle non-finite values.
Results may differ from the reference program's by a relative error of at most 0.0001.
Values sent between devices are 32-bit elements; how exact they have to be, the bound alone decides.
No kernel may reach another device: no remote copies, remote signals or barrier semaphores. Data moves between devices by JAX's collectives and lax.ppermute only.
A program may use at most 64 MiB of HBM per device.

```python
import math
import jax
import jax.numpy as jnp
from jax import lax

M = 512
SEC_DEV = 2
PAIRS_DEV = 4
STEPS = 3
SECTORS = 16
BLOCKS = 32
PAIRS = 128
N_OP = 4


def draw_counts(key, part):
    base_counts = jax.random.randint(jax.random.fold_in(key, 11), (SECTORS,), M // 2, M + 1)
    full_place = jax.random.randint(jax.random.fold_in(key, 12), (), 0, SECTORS)
    offset = jax.random.randint(jax.random.fold_in(key, 13), (), 1, SECTORS)
    small_place = (full_place + offset) % SECTORS
    base_counts = base_counts.at[full_place].set(M)
    base_counts = base_counts.at[small_place].set(M // 2)
    return base_counts.astype(jnp.int32)


def place_ends(entries, stream_key, least, high):
    longest = entries.shape.index(max(entries.shape))
    spots = []
    for shift in (0, 1):
        where = [jax.random.randint(jax.random.fold_in(stream_key, axis), (), 0, length) for axis, length in enumerate(entries.shape)]
        where[longest] = (where[longest] + shift) % entries.shape[longest]
        spots.append(tuple(where))
    return entries.at[spots[0]].set(least).at[spots[1]].set(high)


def block_scale(key, dims, cuts, smallest, largest):
    gain, own = 1.0, jax.random.fold_in(key, 6)
    for dim, blocks in cuts:
        steps = jnp.exp(jax.random.uniform(jax.random.fold_in(own, dim), (blocks,), jnp.float32, smallest / len(cuts), largest / len(cuts)))
        gain = gain * jnp.repeat(steps, dims[dim] // blocks).reshape([-1 if axis == dim else 1 for axis in range(len(dims))])
    return gain


def normal_values(own_key, extent, width, bound, pieces=(), kind=jnp.bfloat16):
    drawn = jax.random.normal(own_key, extent, jnp.float32) * width
    if len(pieces) > 0:
        drawn = block_scale(own_key, extent, pieces, -0.22, 0.18) * drawn
    return jnp.clip(drawn, min=-bound, max=bound).astype(kind)


def setup_inputs(seed: int = 0) -> dict:
    arg_keys = jax.random.split(jax.random.key(seed), 7)
    return {
        "theta": normal_values(arg_keys[0], (SECTORS, M, M), 1.0, 6.0, ((0, 8), (1, 4)), jnp.float32),
        "counts": draw_counts(jax.random.fold_in(arg_keys[6], 71), 0),
        "pair_source": place_ends(jax.random.randint(arg_keys[2], (BLOCKS,), 0, SEC_DEV), jax.random.fold_in(arg_keys[2], 1), 0, SEC_DEV - 1).astype(jnp.int32),
        "pair_target": place_ends(jax.random.randint(arg_keys[3], (BLOCKS,), 0, SECTORS), jax.random.fold_in(arg_keys[3], 1), 0, SECTORS - 1).astype(jnp.int32),
        "left_ops": normal_values(arg_keys[4], (PAIRS, M, M), M ** -0.5, 0.25, ((0, 32),), jnp.float32),
        "right_ops": normal_values(arg_keys[5], (PAIRS, M, M), M ** -0.5, 0.25, ((0, 32),), jnp.float32),
    }


def sector_live(counts):
    positions = jnp.arange(M, dtype=jnp.int32)
    alive = positions[None, :] < counts[:, None]
    return alive[:, :, None] & alive[:, None, :]

def apply_hamiltonian(iterate, live_mask, source_global, pair_target, left_ops, right_ops, factor):

    def add_pair(running, pair_item):
        source, target, left_op, right_op = pair_item
        sector_block = lax.dynamic_index_in_dim(iterate, source, 0, keepdims=False)
        left_product = jnp.dot(left_op, sector_block, precision=lax.Precision.HIGHEST)
        pair_term = jnp.dot(left_product, right_op.T, precision=lax.Precision.HIGHEST)
        return (running.at[target].add(pair_term), None)
    summed, _ = lax.scan(add_pair, jnp.zeros_like(iterate), (source_global, pair_target, left_ops, right_ops))
    return factor * jnp.where(live_mask, summed, jnp.zeros_like(summed))

def reference(theta, counts, pair_source, pair_target, left_ops, right_ops):
    live_mask = sector_live(counts)
    block_of_pair = (jnp.arange(PAIRS, dtype=jnp.int32) // PAIRS_DEV).astype(jnp.int32)
    group_of_block = (jnp.arange(BLOCKS, dtype=jnp.int32) // N_OP).astype(jnp.int32)
    block_source = (group_of_block * SEC_DEV + pair_source).astype(jnp.int32)
    source_global = block_source[block_of_pair].astype(jnp.int32)
    target_global = pair_target[block_of_pair].astype(jnp.int32)
    factor = 0.5 / math.sqrt(N_OP * PAIRS_DEV / SEC_DEV)
    previous = jnp.where(live_mask, theta, jnp.zeros_like(theta))
    current = apply_hamiltonian(previous, live_mask, source_global, target_global, left_ops, right_ops, factor)
    for step_number in range(STEPS - 1):
        following = 2.0 * apply_hamiltonian(current, live_mask, source_global, target_global, left_ops, right_ops, factor) - previous
        previous, current = (current, following)
    return (current, previous)
```

```python
import functools
import math

import jax
import jax.numpy as jnp
from jax import lax
from jax.experimental import pallas as pl
from jax.experimental.pallas import tpu as pltpu
from jax.sharding import PartitionSpec as P

STEPS = 3
CHUNKS = 2
CORES = 2
AXES = ("sec", "op")
MIB = 1 << 20

VMEM = pl.BlockSpec(memory_space=pltpu.VMEM)
SMEM = pl.BlockSpec(memory_space=pltpu.SMEM)


def params(mib):
    return pltpu.CompilerParams(vmem_limit_bytes=mib * MIB)


def partner_of(place, shift, count):
    if count & (count - 1) == 0:
        return place ^ shift
    return (place + shift) % count


def origin_of(place, shift, count):
    if count & (count - 1) == 0:
        return place ^ shift
    return (place + count - shift) % count


def split(value):
    high = value.astype(jnp.bfloat16)
    low = (value - high.astype(jnp.float32)).astype(jnp.bfloat16)
    return high, low


def three_pass(left_high, left_low, right_high, right_low):
    dot = functools.partial(jnp.dot, preferred_element_type=jnp.float32)
    return (
        dot(left_high, right_high)
        + dot(left_high, right_low)
        + dot(left_low, right_high)
    )


def prepare_kernel(left, right, left_high, left_low, right_high, right_low):
    left_high[0], left_low[0] = split(left[0])
    right_high[0], right_low[0] = split(right[0].T)


def prepare(left_ops, right_ops):
    pairs, order, _ = left_ops.shape
    spec = pl.BlockSpec((1, order, order), lambda p: (p, 0, 0))
    part = jax.ShapeDtypeStruct(left_ops.shape, jnp.bfloat16)
    return pl.pallas_call(
        prepare_kernel,
        grid=(pairs,),
        in_specs=[spec] * 2,
        out_specs=[spec] * 4,
        out_shape=[part] * 4,
        compiler_params=params(16),
        cost_estimate=pl.CostEstimate(
            flops=4 * pairs * order * order,
            bytes_accessed=16 * pairs * order * order,
            transcendentals=0,
        ),
        name="prepare",
    )(left_ops, right_ops)


def left_kernel(count, left_high, left_low, *refs):
    parts = refs[:count]
    out_high, out_low, high, low = refs[count:]
    place = lax.axis_index("op")
    rows = parts[0].shape[0]

    @pl.when(pl.program_id(0) == 0)
    def _():
        for shift in range(count):
            start = pl.multiple_of(origin_of(place, shift, count) * rows, rows)
            at = pl.ds(start, rows)
            high[at, :], low[at, :] = split(parts[shift][...])

    product = three_pass(left_high[0], left_low[0], high[...], low[...])
    out_high[0], out_low[0] = split(product)


def left_product(left, parts):
    pairs, order, _ = left[0].shape
    count = len(parts)
    rows, width = parts[0].shape
    op_spec = pl.BlockSpec((1, order, order), lambda p: (p, 0, 0))
    part_spec = pl.BlockSpec((rows, width), lambda p: (0, 0))
    out_spec = pl.BlockSpec((1, order, width), lambda p: (p, 0, 0))
    out = jax.ShapeDtypeStruct((pairs, order, width), jnp.bfloat16)
    return pl.pallas_call(
        functools.partial(left_kernel, count),
        grid=(pairs,),
        in_specs=[op_spec] * 2 + [part_spec] * count,
        out_specs=[out_spec] * 2,
        out_shape=[out] * 2,
        scratch_shapes=[pltpu.VMEM((order, width), jnp.bfloat16)] * 2,
        compiler_params=params(16),
        cost_estimate=pl.CostEstimate(
            flops=6 * pairs * order * order * width,
            bytes_accessed=4 * pairs * order * (order + width),
            transcendentals=0,
        ),
        name="left_product",
    )(*left, *parts)


def right_kernel(count, chunks, right_high, right_low, *refs):
    products = refs[: 2 * chunks]
    outs = refs[2 * chunks : 2 * chunks + count]
    total = refs[2 * chunks + count]
    place = lax.axis_index("op")
    pair = pl.program_id(0)
    width = products[0].shape[2]
    rows = outs[0].shape[0]
    term = None
    for chunk in range(chunks):
        at = pl.ds(chunk * width, width)
        part = three_pass(
            products[2 * chunk][0],
            products[2 * chunk + 1][0],
            right_high[0, at, :],
            right_low[0, at, :],
        )
        term = part if term is None else term + part

    @pl.when(pair == 0)
    def _():
        total[...] = term

    @pl.when(pair > 0)
    def _():
        total[...] += term

    @pl.when(pair == pl.num_programs(0) - 1)
    def _():
        for shift in range(count):
            start = pl.multiple_of(partner_of(place, shift, count) * rows, rows)
            outs[shift][...] = total[pl.ds(start, rows), :]


def right_product(right, products, chunk, count):
    pairs, order, width = products[0].shape
    rows = order // count
    op_spec = pl.BlockSpec((1, order, width), lambda p: (p, 0, chunk))
    product_spec = pl.BlockSpec((1, order, width), lambda p: (p, 0, 0))
    out_spec = pl.BlockSpec((rows, width), lambda p: (0, 0))
    chunks = len(products) // 2
    return pl.pallas_call(
        functools.partial(right_kernel, count, chunks),
        grid=(pairs,),
        in_specs=[op_spec] * 2 + [product_spec] * (2 * chunks),
        out_specs=[out_spec] * count,
        out_shape=[jax.ShapeDtypeStruct((rows, width), jnp.float32)] * count,
        scratch_shapes=[pltpu.VMEM((order, width), jnp.float32)],
        compiler_params=params(16),
        cost_estimate=pl.CostEstimate(
            flops=6 * pairs * order * order * width,
            bytes_accessed=4 * pairs * order * (order + width),
            transcendentals=0,
        ),
        name="right_product",
    )(*right, *products)


def scatter_kernel(count, sec_local, chips, own_target, other_target, *refs):
    own, other, outs, home = (
        refs[:count],
        refs[count],
        refs[count + 1 : count + chips],
        refs[count + chips],
    )
    sec, place = lax.axis_index("sec"), lax.axis_index("op")
    chip, core = lax.div(sec, CORES), lax.rem(sec, CORES)
    sign = 1 - 2 * core
    for out in (*outs, home):
        out[...] = jnp.zeros_like(out)
    for shift in range(count):
        block = origin_of(place, shift, count)
        for target, part in (
            (own_target[block], own[shift]),
            (other_target[block], other.at[shift]),
        ):
            target_sec = lax.div(target, sec_local)
            target_chip = lax.div(target_sec, CORES)
            slot = lax.rem(target, CORES * sec_local)
            distance = (target_chip - chip) * sign
            for step in range(1, chips):

                @pl.when(distance == step)
                def _(part=part, slot=slot, out=outs[step - 1]):
                    out[slot] += part[...]

            @pl.when(target_sec == sec)
            def _(part=part, target=target):
                home[lax.rem(target, sec_local)] += part[...]


def scatter(own_target, other_target, own, other, sec_local, chips):
    rows, width = own[0].shape
    count = len(own)
    far = jax.ShapeDtypeStruct((CORES * sec_local, rows, width), jnp.float32)
    home = jax.ShapeDtypeStruct((sec_local, rows, width), jnp.float32)
    *outs, home = pl.pallas_call(
        functools.partial(scatter_kernel, count, sec_local, chips),
        in_specs=[SMEM] * 2 + [VMEM] * (count + 1),
        out_specs=[VMEM] * chips,
        out_shape=[far] * (chips - 1) + [home],
        compiler_params=params(24),
        cost_estimate=pl.CostEstimate(
            flops=2 * count * rows * width,
            bytes_accessed=4 * rows * width * (4 * count + 4 * chips),
            transcendentals=0,
        ),
        name="scatter",
    )(own_target, other_target, *own, other)
    return outs, home


def gather_kernel(count, home, *refs):
    arrived, send, keep = refs[:count], refs[count], refs[count + 1]
    core = lax.rem(lax.axis_index("sec"), CORES)
    sec_local = home.shape[0]
    for sector in range(sec_local):
        mine = core * sec_local + sector
        theirs = (1 - core) * sec_local + sector
        first, second = arrived[0][theirs], home[sector] + arrived[0][mine]
        for part in arrived[1:]:
            first, second = first + part[theirs], second + part[mine]
        send[sector], keep[sector] = first, second


def gather(home, arrived):
    shape = jax.ShapeDtypeStruct(home.shape, jnp.float32)
    return pl.pallas_call(
        functools.partial(gather_kernel, len(arrived)),
        in_specs=[VMEM] * (1 + len(arrived)),
        out_specs=[VMEM] * 2,
        out_shape=[shape] * 2,
        compiler_params=params(16),
        cost_estimate=pl.CostEstimate(
            flops=home.size * 2 * len(arrived),
            bytes_accessed=home.size * 4 * (2 * len(arrived) + 3),
            transcendentals=0,
        ),
        name="gather",
    )(home, *arrived)


def finish_kernel(count, terms, scale, subtract, chunk, counts, source, *refs):
    summands, refs = refs[:terms], refs[terms:]
    if subtract:
        before, refs = refs[0], refs[1:]
    new, parts = refs[0], refs[1:]
    place = lax.axis_index("op")
    sec_local, rows, width = new.shape
    row = place * rows + lax.broadcasted_iota(jnp.int32, (rows, width), 0)
    column = chunk * width + lax.broadcasted_iota(jnp.int32, (rows, width), 1)
    for sector in range(sec_local):
        value = summands[0][sector]
        for summand in summands[1:]:
            value = value + summand[sector]
        live = (row < counts[sector]) & (column < counts[sector])
        value = jnp.where(live, scale * value, 0.0)
        if subtract:
            value = value - before[sector]
        new[sector] = value
    for shift in range(len(parts)):
        parts[shift][...] = new[source[partner_of(place, shift, count)]]


def finish(counts, source, summands, before, scale, chunk, chunks, send):
    sec_local, rows, width = summands[0].shape
    count = source.shape[0]
    whole = pl.BlockSpec((sec_local, rows, width), lambda i: (0, 0, 0))
    if chunks:
        width //= chunks
        whole = pl.BlockSpec((sec_local, rows, width), lambda i: (0, 0, chunk))
    spec = pl.BlockSpec((sec_local, rows, width), lambda i: (0, 0, 0))
    part_spec = pl.BlockSpec((rows, width), lambda i: (0, 0))
    operands = (*summands, *(() if before is None else (before,)))
    parts = count if send else 0
    return pl.pallas_call(
        functools.partial(
            finish_kernel,
            count,
            len(summands),
            scale,
            before is not None,
            chunk,
        ),
        grid=(1,),
        in_specs=[SMEM] * 2 + [whole if chunks else spec] * len(operands),
        out_specs=[spec] + [part_spec] * parts,
        out_shape=[jax.ShapeDtypeStruct((sec_local, rows, width), jnp.float32)]
        + [jax.ShapeDtypeStruct((rows, width), jnp.float32)] * parts,
        compiler_params=params(16),
        cost_estimate=pl.CostEstimate(
            flops=4 * sec_local * rows * width,
            bytes_accessed=4 * rows * width * (sec_local * 4 + parts),
            transcendentals=0,
        ),
        name="finish",
    )(counts, source, *operands)


def per_device(shape, theta, counts, source, target, left_ops, right_ops):
    secs, ops = shape["sec"], shape["op"]
    chips = secs // CORES
    sec_local, rows, order = theta.shape
    pairs = left_ops.shape[0]
    factor = 0.5 / math.sqrt(target.shape[0] * pairs / sec_local)

    def permute(value, where):
        pairs = []
        for sec in range(secs):
            for op in range(ops):
                to = where(sec, op)
                if to is not None:
                    pairs.append((sec * ops + op, to[0] * ops + to[1]))
        return lax.ppermute(value, AXES, pairs)

    def to_core(value):
        return permute(value, lambda sec, op: (sec ^ 1, op))

    def to_partners(parts):
        return [parts[0]] + [
            permute(
                parts[shift],
                lambda sec, op, shift=shift: (sec, partner_of(op, shift, ops)),
            )
            for shift in range(1, ops)
        ]

    def along(value, distance, levels):
        def where(sec, op):
            chip, core = sec // CORES, sec % CORES
            level = chip if core == 0 else chips - 1 - chip
            to = chip + (distance if core == 0 else -distance)
            if level in levels and level + distance < chips:
                return to * CORES + core, op
            return None

        return permute(value, where)

    other_target = to_core(target)
    left = None

    def sums(pieces):
        own = to_partners(pieces)
        other = to_core(jnp.stack(own))
        outs, home = scatter(target, other_target, own, other, sec_local, chips)
        arrived = []
        every = set(range(chips))
        relay = None
        if chips > 2:
            relay = along(outs[1], 1, {0})
        for distance in range(chips - 1, 1, -1):
            levels = every - {0} if distance == 2 else every
            if any(level + distance < chips for level in levels):
                arrived.append(along(outs[distance - 1], distance, levels))
        if chips > 1:
            last = outs[0] if relay is None else outs[0] + relay
            arrived.append(along(last, 1, every))
        if not arrived:
            return (home,)
        give, keep = gather(home, arrived)
        return keep, to_core(give)

    before = [None] * CHUNKS
    now, parts = [], []
    for chunk in range(CHUNKS):
        new, *send = finish(counts, source, (theta,), None, 1.0, chunk, CHUNKS, True)
        now.append(new)
        parts.append(to_partners(send))
    left_high, left_low, right_high, right_low = prepare(left_ops, right_ops)
    left, right = (left_high, left_low), (right_high, right_low)
    for step in range(STEPS):
        products = []
        for chunk in range(CHUNKS):
            products.extend(left_product(left, parts[chunk]))
        parts, after = [], []
        for chunk in range(CHUNKS):
            pieces = right_product(right, products, chunk, ops)
            new, *send = finish(
                counts,
                source,
                sums(pieces),
                before[chunk],
                factor if step == 0 else 2.0 * factor,
                chunk,
                0,
                step < STEPS - 1,
            )
            after.append(new)
            if send:
                parts.append(to_partners(send))
        before, now = now, after
    return jnp.concatenate(now, axis=2), jnp.concatenate(before, axis=2)


def solution(mesh):
    in_specs = (
        P("sec", "op", None),
        P("sec"),
        P("sec"),
        P("sec"),
        P(("sec", "op"), None, None),
        P(("sec", "op"), None, None),
    )
    out_specs = (P("sec", "op", None), P("sec", "op", None))
    return jax.shard_map(
        functools.partial(per_device, dict(mesh.shape)),
        mesh=mesh,
        in_specs=in_specs,
        out_specs=out_specs,
        check_vma=False,
    )
```

```python
import functools
import math

import jax
import jax.numpy as jnp
from jax import lax
from jax.experimental import pallas as pl
from jax.experimental.pallas import tpu as pltpu
from jax.sharding import PartitionSpec as P


STEPS = 3
CHUNKS = 2
CORES = 2
AXES = ("sec", "op")
MIB = 1 << 20

VMEM = pl.BlockSpec(memory_space=pltpu.VMEM)
SMEM = pl.BlockSpec(memory_space=pltpu.SMEM)


def params(mib):
    return pltpu.CompilerParams(vmem_limit_bytes=mib * MIB)


def partner_of(place, shift, count):
    if count & (count - 1) == 0:
        return place ^ shift
    return (place + shift) % count


def origin_of(place, shift, count):
    if count & (count - 1) == 0:
        return place ^ shift
    return (place + count - shift) % count


def split(value):
    high = value.astype(jnp.bfloat16)
    low = (value - high.astype(jnp.float32)).astype(jnp.bfloat16)
    return high, low


def three_pass(left_high, left_low, right_high, right_low):
    dot = functools.partial(jnp.dot, preferred_element_type=jnp.float32)
    return (
        dot(left_high, right_high)
        + dot(left_high, right_low)
        + dot(left_low, right_high)
    )


def prepare_kernel(left, right, left_high, left_low, right_high, right_low):
    left_high[0], left_low[0] = split(left[0])
    right_high[0], right_low[0] = split(right[0].T)


def prepare(left_ops, right_ops):
    pairs, order, _ = left_ops.shape
    spec = pl.BlockSpec((1, order, order), lambda p: (p, 0, 0))
    part = jax.ShapeDtypeStruct(left_ops.shape, jnp.bfloat16)
    return pl.pallas_call(
        prepare_kernel,
        grid=(pairs,),
        in_specs=[spec] * 2,
        out_specs=[spec] * 4,
        out_shape=[part] * 4,
        compiler_params=params(16),
        cost_estimate=pl.CostEstimate(
            flops=4 * pairs * order * order,
            bytes_accessed=16 * pairs * order * order,
            transcendentals=0,
        ),
        name="prepare",
    )(left_ops, right_ops)


def left_kernel(count, left_high, left_low, *refs):
    parts = refs[:count]
    out_high, out_low, high, low = refs[count:]
    place = lax.axis_index("op")
    rows = parts[0].shape[0]

    @pl.when(pl.program_id(0) == 0)
    def _():
        for shift in range(count):
            start = pl.multiple_of(origin_of(place, shift, count) * rows, rows)
            at = pl.ds(start, rows)
            high[at, :], low[at, :] = split(parts[shift][...])

    product = three_pass(left_high[0], left_low[0], high[...], low[...])
    out_high[0], out_low[0] = split(product)


def left_product(left, parts):
    pairs, order, _ = left[0].shape
    count = len(parts)
    rows, width = parts[0].shape
    op_spec = pl.BlockSpec((1, order, order), lambda p: (p, 0, 0))
    part_spec = pl.BlockSpec((rows, width), lambda p: (0, 0))
    out_spec = pl.BlockSpec((1, order, width), lambda p: (p, 0, 0))
    out = jax.ShapeDtypeStruct((pairs, order, width), jnp.bfloat16)
    return pl.pallas_call(
        functools.partial(left_kernel, count),
        grid=(pairs,),
        in_specs=[op_spec] * 2 + [part_spec] * count,
        out_specs=[out_spec] * 2,
        out_shape=[out] * 2,
        scratch_shapes=[pltpu.VMEM((order, width), jnp.bfloat16)] * 2,
        compiler_params=params(16),
        cost_estimate=pl.CostEstimate(
            flops=6 * pairs * order * order * width,
            bytes_accessed=4 * pairs * order * (order + width),
            transcendentals=0,
        ),
        name="left_product",
    )(*left, *parts)


def right_kernel(count, chunks, right_high, right_low, *refs):
    products = refs[: 2 * chunks]
    outs = refs[2 * chunks : 2 * chunks + count]
    total = refs[2 * chunks + count]
    place = lax.axis_index("op")
    pair = pl.program_id(0)
    width = products[0].shape[2]
    rows = outs[0].shape[0]
    term = None
    for chunk in range(chunks):
        at = pl.ds(chunk * width, width)
        part = three_pass(
            products[2 * chunk][0],
            products[2 * chunk + 1][0],
            right_high[0, at, :],
            right_low[0, at, :],
        )
        term = part if term is None else term + part

    @pl.when(pair == 0)
    def _():
        total[...] = term

    @pl.when(pair > 0)
    def _():
        total[...] += term

    @pl.when(pair == pl.num_programs(0) - 1)
    def _():
        for shift in range(count):
            start = pl.multiple_of(partner_of(place, shift, count) * rows, rows)
            outs[shift][...] = total[pl.ds(start, rows), :]


def right_product(right, products, chunk, count):
    pairs, order, width = products[0].shape
    rows = order // count
    op_spec = pl.BlockSpec((1, order, width), lambda p: (p, 0, chunk))
    product_spec = pl.BlockSpec((1, order, width), lambda p: (p, 0, 0))
    out_spec = pl.BlockSpec((rows, width), lambda p: (0, 0))
    chunks = len(products) // 2
    return pl.pallas_call(
        functools.partial(right_kernel, count, chunks),
        grid=(pairs,),
        in_specs=[op_spec] * 2 + [product_spec] * (2 * chunks),
        out_specs=[out_spec] * count,
        out_shape=[jax.ShapeDtypeStruct((rows, width), jnp.float32)] * count,
        scratch_shapes=[pltpu.VMEM((order, width), jnp.float32)],
        compiler_params=params(16),
        cost_estimate=pl.CostEstimate(
            flops=6 * pairs * order * order * width,
            bytes_accessed=4 * pairs * order * (order + width),
            transcendentals=0,
        ),
        name="right_product",
    )(*right, *products)


def scatter_kernel(count, sec_local, chips, own_target, other_target, *refs):
    own, other, outs, home = (
        refs[:count],
        refs[count],
        refs[count + 1 : count + chips],
        refs[count + chips],
    )
    sec, place = lax.axis_index("sec"), lax.axis_index("op")
    chip, core = lax.div(sec, CORES), lax.rem(sec, CORES)
    sign = 1 - 2 * core
    for out in (*outs, home):
        out[...] = jnp.zeros_like(out)
    for shift in range(count):
        block = origin_of(place, shift, count)
        for target, part in (
            (own_target[block], own[shift]),
            (other_target[block], other.at[shift]),
        ):
            target_sec = lax.div(target, sec_local)
            target_chip = lax.div(target_sec, CORES)
            slot = lax.rem(target, CORES * sec_local)
            distance = (target_chip - chip) * sign
            for step in range(1, chips):

                @pl.when(distance == step)
                def _(part=part, slot=slot, out=outs[step - 1]):
                    out[slot] += part[...]

            @pl.when(target_sec == sec)
            def _(part=part, target=target):
                home[lax.rem(target, sec_local)] += part[...]


def scatter(own_target, other_target, own, other, sec_local, chips):
    rows, width = own[0].shape
    count = len(own)
    far = jax.ShapeDtypeStruct((CORES * sec_local, rows, width), jnp.float32)
    home = jax.ShapeDtypeStruct((sec_local, rows, width), jnp.float32)
    *outs, home = pl.pallas_call(
        functools.partial(scatter_kernel, count, sec_local, chips),
        in_specs=[SMEM] * 2 + [VMEM] * (count + 1),
        out_specs=[VMEM] * chips,
        out_shape=[far] * (chips - 1) + [home],
        compiler_params=params(24),
        cost_estimate=pl.CostEstimate(
            flops=2 * count * rows * width,
            bytes_accessed=4 * rows * width * (4 * count + 4 * chips),
            transcendentals=0,
        ),
        name="scatter",
    )(own_target, other_target, *own, other)
    return outs, home


def gather_kernel(count, home, *refs):
    arrived, send, keep = refs[:count], refs[count], refs[count + 1]
    core = lax.rem(lax.axis_index("sec"), CORES)
    sec_local = home.shape[0]
    for sector in range(sec_local):
        mine = core * sec_local + sector
        theirs = (1 - core) * sec_local + sector
        first, second = arrived[0][theirs], home[sector] + arrived[0][mine]
        for part in arrived[1:]:
            first, second = first + part[theirs], second + part[mine]
        send[sector], keep[sector] = first, second


def gather(home, arrived):
    shape = jax.ShapeDtypeStruct(home.shape, jnp.float32)
    return pl.pallas_call(
        functools.partial(gather_kernel, len(arrived)),
        in_specs=[VMEM] * (1 + len(arrived)),
        out_specs=[VMEM] * 2,
        out_shape=[shape] * 2,
        compiler_params=params(16),
        cost_estimate=pl.CostEstimate(
            flops=home.size * 2 * len(arrived),
            bytes_accessed=home.size * 4 * (2 * len(arrived) + 3),
            transcendentals=0,
        ),
        name="gather",
    )(home, *arrived)


def finish_kernel(count, terms, scale, subtract, chunk, counts, source, *refs):
    summands, refs = refs[:terms], refs[terms:]
    if subtract:
        before, refs = refs[0], refs[1:]
    new, parts = refs[0], refs[1:]
    place = lax.axis_index("op")
    sec_local, rows, width = new.shape
    row = place * rows + lax.broadcasted_iota(jnp.int32, (rows, width), 0)
    column = chunk * width + lax.broadcasted_iota(jnp.int32, (rows, width), 1)
    for sector in range(sec_local):
        value = summands[0][sector]
        for summand in summands[1:]:
            value = value + summand[sector]
        live = (row < counts[sector]) & (column < counts[sector])
        value = jnp.where(live, scale * value, 0.0)
        if subtract:
            value = value - before[sector]
        new[sector] = value
    for shift in range(len(parts)):
        parts[shift][...] = new[source[partner_of(place, shift, count)]]


def finish(counts, source, summands, before, scale, chunk, chunks, send):
    sec_local, rows, width = summands[0].shape
    count = source.shape[0]
    whole = pl.BlockSpec((sec_local, rows, width), lambda i: (0, 0, 0))
    if chunks:
        width //= chunks
        whole = pl.BlockSpec((sec_local, rows, width), lambda i: (0, 0, chunk))
    spec = pl.BlockSpec((sec_local, rows, width), lambda i: (0, 0, 0))
    part_spec = pl.BlockSpec((rows, width), lambda i: (0, 0))
    operands = (*summands, *(() if before is None else (before,)))
    parts = count if send else 0
    return pl.pallas_call(
        functools.partial(
            finish_kernel,
            count,
            len(summands),
            scale,
            before is not None,
            chunk,
        ),
        grid=(1,),
        in_specs=[SMEM] * 2 + [whole if chunks else spec] * len(operands),
        out_specs=[spec] + [part_spec] * parts,
        out_shape=[jax.ShapeDtypeStruct((sec_local, rows, width), jnp.float32)]
        + [jax.ShapeDtypeStruct((rows, width), jnp.float32)] * parts,
        compiler_params=params(16),
        cost_estimate=pl.CostEstimate(
            flops=4 * sec_local * rows * width,
            bytes_accessed=4 * rows * width * (sec_local * 4 + parts),
            transcendentals=0,
        ),
        name="finish",
    )(counts, source, *operands)


def per_device(shape, theta, counts, source, target, left_ops, right_ops):
    secs, ops = shape["sec"], shape["op"]
    chips = secs // CORES
    sec_local, _, _ = theta.shape
    pairs = left_ops.shape[0]
    factor = 0.5 / math.sqrt(target.shape[0] * pairs / sec_local)

    def permute(value, where):
        pairs = []
        for sec in range(secs):
            for op in range(ops):
                to = where(sec, op)
                if to is not None:
                    pairs.append((sec * ops + op, to[0] * ops + to[1]))
        return lax.ppermute(value, AXES, pairs)

    def to_core(value):
        return permute(value, lambda sec, op: (sec ^ 1, op))

    def to_partners(parts):
        here = [parts[0]]
        for shift in range(1, ops):
            here.append(
                permute(
                    parts[shift],
                    lambda sec, op: (sec, partner_of(op, shift, ops)),
                )
            )
        return here

    def along(value, distance, levels):
        def where(sec, op):
            chip, core = sec // CORES, sec % CORES
            level = chip if core == 0 else chips - 1 - chip
            to = chip + (distance if core == 0 else -distance)
            if level in levels and level + distance < chips:
                return to * CORES + core, op
            return None

        return permute(value, where)

    other_target = to_core(target)

    def sums(pieces):
        own = to_partners(pieces)
        other = to_core(jnp.stack(own))
        outs, home = scatter(target, other_target, own, other, sec_local, chips)
        arrived = []
        every = set(range(chips))
        relay = None
        if chips > 2:
            relay = along(outs[1], 1, {0})
        for distance in range(2, chips):
            levels = every - {0} if distance == 2 else every
            if any(level + distance < chips for level in levels):
                arrived.append(along(outs[distance - 1], distance, levels))
        if chips > 1:
            last = outs[0] if relay is None else outs[0] + relay
            arrived.append(along(last, 1, every))
        if not arrived:
            return (home,)
        give, keep = gather(home, arrived)
        return keep, to_core(give)

    before = [None] * CHUNKS
    now, parts = [], []
    for chunk in range(CHUNKS):
        new, *send = finish(
            counts, source, (theta,), None, 1.0, chunk, CHUNKS, True
        )
        now.append(new)
        parts.append(to_partners(send))
    prepared = prepare(left_ops, right_ops)
    left, right = prepared[:2], prepared[2:]
    products = []
    for chunk in range(CHUNKS):
        products.extend(left_product(left, parts[chunk]))
    for step in range(STEPS):
        parts, after = [], []
        for chunk in range(CHUNKS):
            pieces = right_product(right, products, chunk, ops)
            terms = sums(pieces)
            new, *send = finish(
                counts,
                source,
                terms,
                before[chunk],
                factor if step == 0 else 2.0 * factor,
                chunk,
                0,
                step < STEPS - 1,
            )
            after.append(new)
            if send:
                parts.append(to_partners(send))
        before, now, products = now, after, []
        for chunk in range(len(parts)):
            products.extend(left_product(left, parts[chunk]))
    return jnp.concatenate(now, axis=2), jnp.concatenate(before, axis=2)


def solution(mesh):
    in_specs = (
        P("sec", "op", None),
        P("sec"),
        P("sec"),
        P("sec"),
        P(("sec", "op"), None, None),
        P(("sec", "op"), None, None),
    )
    out_specs = (P("sec", "op", None), P("sec", "op", None))
    return jax.shard_map(
        functools.partial(per_device, dict(mesh.shape)),
        mesh=mesh,
        in_specs=in_specs,
        out_specs=out_specs,
        check_vma=False,
    )
```

```python
import functools
import math

import jax
import jax.numpy as jnp
from jax import lax
from jax.experimental import pallas as pl
from jax.experimental.pallas import tpu as pltpu
from jax.sharding import PartitionSpec as P


STEPS = 3
CORES = 2
LANES = 128
AXES = ("sec", "op")
MIB = 1 << 20

VMEM = pl.BlockSpec(memory_space=pltpu.VMEM)
SMEM = pl.BlockSpec(memory_space=pltpu.SMEM)


def params(mib):
    return pltpu.CompilerParams(vmem_limit_bytes=mib * MIB)


def partner_of(place, shift, count):
    if count & (count - 1) == 0:
        return place ^ shift
    return (place + shift) % count


def origin_of(place, shift, count):
    if count & (count - 1) == 0:
        return place ^ shift
    return (place + count - shift) % count


def split(value):
    high = value.astype(jnp.bfloat16)
    low = (value - high.astype(jnp.float32)).astype(jnp.bfloat16)
    return high, low


def widths_of(order):
    if order % (2 * LANES):
        return (order,)
    return (order // 2, order // 2)


def starts_of(widths):
    return [sum(widths[:chunk]) for chunk in range(len(widths))]


def three_pass(left_high, left_low, right_high, right_low):
    dot = functools.partial(jnp.dot, preferred_element_type=jnp.float32)
    return (
        dot(left_high, right_high)
        + dot(left_high, right_low)
        + dot(left_low, right_high)
    )


def prepare_kernel(widths, left, right, left_high, left_low, *rights):
    left_high[0], left_low[0] = split(left[0])
    turned = right[0].T
    for chunk, (start, width) in enumerate(zip(starts_of(widths), widths)):
        part = turned[:, start : start + width]
        rights[2 * chunk][0], rights[2 * chunk + 1][0] = split(part)


def prepare(left_ops, right_ops, widths):
    pairs, order, _ = left_ops.shape

    def spec(width):
        return pl.BlockSpec((1, order, width), lambda p: (p, 0, 0))

    outs = [order] * 2 + [width for width in widths for _ in range(2)]
    high_low = pl.pallas_call(
        functools.partial(prepare_kernel, widths),
        grid=(pairs,),
        in_specs=[spec(order)] * 2,
        out_specs=[spec(width) for width in outs],
        out_shape=[
            jax.ShapeDtypeStruct((pairs, order, width), jnp.bfloat16) for width in outs
        ],
        compiler_params=params(16),
        cost_estimate=pl.CostEstimate(
            flops=4 * pairs * order * order,
            bytes_accessed=16 * pairs * order * order,
            transcendentals=0,
        ),
        name="prepare",
    )(left_ops, right_ops)
    pairs = list(zip(high_low[::2], high_low[1::2]))
    return pairs[0], pairs[1:]


def left_kernel(count, carried, last, start, *refs):
    left_high, left_low, right_high, right_low = refs[:4]
    parts, refs = refs[4 : 4 + count], refs[4 + count :]
    before, refs = refs[:carried], refs[carried:]
    out_high, out_low = refs[:2]
    outs, (high, low, total) = refs[2:-3], refs[-3:]
    place, pair = lax.axis_index("op"), pl.program_id(0)
    rows, width = parts[0].shape

    @pl.when(pair == 0)
    def _():
        for shift in range(count):
            at = pl.ds(pl.multiple_of(origin_of(place, shift, count) * rows, rows), rows)
            high[at, :], low[at, :] = split(parts[shift][...])
        total[...] = before[0][...] if carried else jnp.zeros_like(total)

    product = three_pass(left_high[0], left_low[0], high[...], low[...])
    product_high, product_low = split(product)
    out_high[0], out_low[0] = product_high, product_low
    at = pl.ds(start, width)
    total[...] += three_pass(
        product_high, product_low, right_high[0, at, :], right_low[0, at, :]
    )

    @pl.when(pair == pl.num_programs(0) - 1)
    def _():
        if last:
            put_rows(total, outs, place)
        else:
            outs[0][...] = total[...]


def put_rows(total, outs, place):
    count, rows = len(outs), outs[0].shape[0]
    for shift in range(count):
        start = pl.multiple_of(partner_of(place, shift, count) * rows, rows)
        outs[shift][...] = total[pl.ds(start, rows), :]


def left_product(left, right, parts, before, start, last):
    pairs, order, _ = left[0].shape
    count = len(parts)
    rows, width = parts[0].shape
    first = right[0].shape[2]

    def by_pair(width):
        return pl.BlockSpec((1, order, width), lambda p: (p, 0, 0))

    def whole(rows, width):
        return pl.BlockSpec((rows, width), lambda p: (0, 0))

    out = jax.ShapeDtypeStruct((pairs, order, width), jnp.bfloat16)
    pieces, height = (count, rows) if last else (1, order)
    high, low, *sums = pl.pallas_call(
        functools.partial(left_kernel, count, len(before), last, start),
        grid=(pairs,),
        in_specs=[by_pair(order)] * 2
        + [by_pair(first)] * 2
        + [whole(rows, width)] * count
        + [whole(order, first)] * len(before),
        out_specs=[by_pair(width)] * 2 + [whole(height, first)] * pieces,
        out_shape=[out] * 2
        + [jax.ShapeDtypeStruct((height, first), jnp.float32)] * pieces,
        scratch_shapes=[pltpu.VMEM((order, width), jnp.bfloat16)] * 2
        + [pltpu.VMEM((order, first), jnp.float32)],
        compiler_params=params(16),
        cost_estimate=pl.CostEstimate(
            flops=6 * pairs * order * width * (order + first),
            bytes_accessed=4 * pairs * order * (order + width + first),
            transcendentals=0,
        ),
        name="left_product",
    )(*left, *right, *parts, *before)
    return (high, low), sums


def right_kernel(count, chunks, right_high, right_low, *refs):
    products = refs[: 2 * chunks]
    outs = refs[2 * chunks : 2 * chunks + count]
    total = refs[2 * chunks + count]
    place = lax.axis_index("op")
    pair = pl.program_id(0)
    term, start = 0.0, 0
    for high, low in zip(products[::2], products[1::2]):
        at = pl.ds(start, high.shape[2])
        right = right_high[0, at, :], right_low[0, at, :]
        term = term + three_pass(high[0], low[0], *right)
        start += high.shape[2]

    @pl.when(pair == 0)
    def _():
        total[...] = term

    @pl.when(pair > 0)
    def _():
        total[...] += term

    @pl.when(pair == pl.num_programs(0) - 1)
    def _():
        put_rows(total, outs, place)


def right_product(right, products, count):
    pairs, order, width = right[0].shape
    rows = order // count

    def spec(width):
        return pl.BlockSpec((1, order, width), lambda p: (p, 0, 0))

    out_spec = pl.BlockSpec((rows, width), lambda p: (0, 0))
    return pl.pallas_call(
        functools.partial(right_kernel, count, len(products) // 2),
        grid=(pairs,),
        in_specs=[spec(part.shape[2]) for part in (*right, *products)],
        out_specs=[out_spec] * count,
        out_shape=[jax.ShapeDtypeStruct((rows, width), jnp.float32)] * count,
        scratch_shapes=[pltpu.VMEM((order, width), jnp.float32)],
        compiler_params=params(16),
        cost_estimate=pl.CostEstimate(
            flops=6 * pairs * order * order * width,
            bytes_accessed=4 * pairs * order * (order + width),
            transcendentals=0,
        ),
        name="right_product",
    )(*right, *products)


def scatter_kernel(count, sec_local, chips, own_target, other_target, *refs):
    own, other, outs, home = (
        refs[:count],
        refs[count],
        refs[count + 1 : count + chips],
        refs[count + chips],
    )
    sec, place = lax.axis_index("sec"), lax.axis_index("op")
    chip, core = lax.div(sec, CORES), lax.rem(sec, CORES)
    sign = 1 - 2 * core
    for out in (*outs, home):
        out[...] = jnp.zeros_like(out)
    for shift in range(count):
        block = origin_of(place, shift, count)
        for target, part in (
            (own_target[block], own[shift]),
            (other_target[block], other.at[shift]),
        ):
            target_sec = lax.div(target, sec_local)
            target_chip = lax.div(target_sec, CORES)
            slot = lax.rem(target, CORES * sec_local)
            distance = (target_chip - chip) * sign
            for step in range(1, chips):

                @pl.when(distance == step)
                def _(part=part, slot=slot, out=outs[step - 1]):
                    out[slot] += part[...]

            @pl.when(target_sec == sec)
            def _(part=part, target=target):
                home[lax.rem(target, sec_local)] += part[...]


def scatter(own_target, other_target, own, other, sec_local, chips):
    rows, width = own[0].shape
    count = len(own)
    far = jax.ShapeDtypeStruct((CORES * sec_local, rows, width), jnp.float32)
    home = jax.ShapeDtypeStruct((sec_local, rows, width), jnp.float32)
    *outs, home = pl.pallas_call(
        functools.partial(scatter_kernel, count, sec_local, chips),
        in_specs=[SMEM] * 2 + [VMEM] * (count + 1),
        out_specs=[VMEM] * chips,
        out_shape=[far] * (chips - 1) + [home],
        compiler_params=params(16),
        cost_estimate=pl.CostEstimate(
            flops=2 * count * rows * width,
            bytes_accessed=4 * rows * width * (4 * count + 4 * chips),
            transcendentals=0,
        ),
        name="scatter",
    )(own_target, other_target, *own, other)
    return outs, home


def level_of(chips):
    sec = lax.axis_index("sec")
    chip, core = lax.div(sec, CORES), lax.rem(sec, CORES)
    return jnp.where(core == 0, chip, chips - 1 - chip)


def merge_kernel(chips, near, *refs):
    relayed, same, cross = refs[:-2], refs[-2], refs[-1]
    core = lax.rem(lax.axis_index("sec"), CORES)
    sec_local = same.shape[0]
    relays = level_of(chips) == 1 if relayed else None
    for out, owner in ((same, core), (cross, 1 - core)):
        for sector in range(sec_local):
            at = owner * sec_local + sector
            value = near[at]
            for part in relayed:
                value = value + jnp.where(relays, part[at], 0.0)
            out[sector] = value


def merge(near, relayed, chips):
    sectors, rows, width = near.shape
    half = jax.ShapeDtypeStruct((sectors // CORES, rows, width), jnp.float32)
    return pl.pallas_call(
        functools.partial(merge_kernel, chips),
        in_specs=[VMEM] * (1 + len(relayed)),
        out_specs=[VMEM] * 2,
        out_shape=[half] * 2,
        compiler_params=params(16),
        cost_estimate=pl.CostEstimate(
            flops=near.size, bytes_accessed=12 * near.size, transcendentals=0
        ),
        name="merge",
    )(near, *relayed)


def gather_kernel(chips, home, *refs):
    arrived, send, keep = refs[:-2], refs[-2], refs[-1]
    core = lax.rem(lax.axis_index("sec"), CORES)
    relays = level_of(chips) == 1
    sec_local = home.shape[0]
    for sector in range(sec_local):
        mine = core * sec_local + sector
        theirs = (1 - core) * sec_local + sector
        first = jnp.where(relays, 0.0, arrived[0][theirs])
        second = jnp.where(relays, 0.0, arrived[0][mine])
        for part in arrived[1:]:
            first, second = first + part[theirs], second + part[mine]
        send[sector], keep[sector] = first, home[sector] + second


def gather(home, arrived, chips):
    shape = jax.ShapeDtypeStruct(home.shape, jnp.float32)
    return pl.pallas_call(
        functools.partial(gather_kernel, chips),
        in_specs=[VMEM] * (1 + len(arrived)),
        out_specs=[VMEM] * 2,
        out_shape=[shape] * 2,
        compiler_params=params(16),
        cost_estimate=pl.CostEstimate(
            flops=home.size * 2 * len(arrived),
            bytes_accessed=home.size * 4 * (2 * len(arrived) + 3),
            transcendentals=0,
        ),
        name="gather",
    )(home, *arrived)


def finish(counts, source, summands, before, scale, start, width, send):
    sec_local, rows, _ = summands[0].shape
    count = source.shape[0]
    terms, parts = len(summands), count if send else 0

    def kernel(counts, source, *refs):
        old = refs[terms : len(refs) - 1 - parts]
        new = refs[len(refs) - 1 - parts]
        outs = refs[len(refs) - parts :]
        place = lax.axis_index("op")
        row = place * rows + lax.broadcasted_iota(jnp.int32, (rows, width), 0)
        column = start + lax.broadcasted_iota(jnp.int32, (rows, width), 1)
        for sector in range(sec_local):
            value = None
            for summand in refs[:terms]:
                if summand.shape[2] == width:
                    part = summand[sector]
                else:
                    part = summand[sector, :, start : start + width]
                value = part if value is None else value + part
            live = (row < counts[sector]) & (column < counts[sector])
            value = jnp.where(live, scale * value, 0.0)
            for part in old:
                value = value - part[sector]
            new[sector] = value
        for shift in range(parts):
            outs[shift][...] = new[source[partner_of(place, shift, count)]]

    operands = (*summands, *(() if before is None else (before,)))

    def whole(shape):
        return pl.BlockSpec(shape, lambda i: (0,) * len(shape))

    new = (sec_local, rows, width)
    return pl.pallas_call(
        kernel,
        grid=(1,),
        in_specs=[SMEM] * 2 + [whole(operand.shape) for operand in operands],
        out_specs=[whole(new)] + [whole(new[1:])] * parts,
        out_shape=[jax.ShapeDtypeStruct((sec_local, rows, width), jnp.float32)]
        + [jax.ShapeDtypeStruct((rows, width), jnp.float32)] * parts,
        compiler_params=params(16),
        cost_estimate=pl.CostEstimate(
            flops=4 * sec_local * rows * width,
            bytes_accessed=4 * rows * width * (sec_local * 4 + parts),
            transcendentals=0,
        ),
        name="finish",
    )(counts, source, *operands)


def per_device(shape, theta, counts, source, target, left_ops, right_ops):
    secs, ops = shape["sec"], shape["op"]
    chips = secs // CORES
    sec_local, _, order = theta.shape
    pairs = left_ops.shape[0]
    factor = 0.5 / math.sqrt(target.shape[0] * pairs / sec_local)

    def permute(value, where):
        pairs = []
        for sec in range(secs):
            for op in range(ops):
                to = where(sec, op)
                if to is not None:
                    pairs.append((sec * ops + op, to[0] * ops + to[1]))
        return lax.ppermute(value, AXES, pairs)

    def to_core(value):
        return permute(value, lambda sec, op: (sec ^ 1, op))

    def to_partners(parts):
        here = [parts[0]]
        for shift in range(1, ops):
            here.append(
                permute(
                    parts[shift],
                    lambda sec, op: (sec, partner_of(op, shift, ops)),
                )
            )
        return here

    def along(value, steps, cross=0):
        def where(sec, op):
            chip, core = sec // CORES, sec % CORES
            level = chip if core == 0 else chips - 1 - chip
            if level not in steps or level + steps[level] >= chips:
                return None
            to = chip + (steps[level] if core == 0 else -steps[level])
            return to * CORES + (core ^ cross), op

        return permute(value, where)

    other_target = to_core(target)

    def sums(pieces):
        own = to_partners(pieces)
        other = to_core(jnp.stack(own))
        outs, home = scatter(target, other_target, own, other, sec_local, chips)
        arrived = []
        if chips > 2:
            steps = {level: 2 for level in range(1, chips)} | {0: 1}
            arrived.append(along(outs[1], steps))
        for distance in range(3, chips):
            steps = {level: distance for level in range(chips)}
            arrived.append(along(outs[distance - 1], steps))
        terms = [home]
        if arrived:
            give, keep = gather(home, arrived, chips)
            terms = [keep, to_core(give)]
        if chips > 1:
            halves = merge(outs[0], arrived[:1], chips)
            one = {level: 1 for level in range(chips)}
            for cross, half in enumerate(halves):
                terms.append(along(half, one, cross))
        return terms

    widths = widths_of(order)
    starts = starts_of(widths)
    chunks = range(len(widths))
    before = [None] * len(widths)

    def left_products(parts):
        products, carry = [], []
        for chunk in chunks:
            product, carry = left_product(
                left,
                right[0],
                parts[chunk],
                carry,
                starts[chunk],
                chunk == chunks[-1],
            )
            products.extend(product)
        return products, carry

    now, parts = [], []
    for chunk in chunks:
        new, *send = finish(
            counts,
            source,
            (theta,),
            None,
            1.0,
            starts[chunk],
            widths[chunk],
            True,
        )
        now.append(new)
        parts.append(to_partners(send))
    left, right = prepare(left_ops, right_ops, widths)
    products, first = left_products(parts)

    for step in range(STEPS):
        parts, after = [], []
        for chunk in chunks:
            if chunk == 0:
                pieces = first
            else:
                pieces = right_product(right[chunk], products, ops)
            terms = sums(pieces)
            new, *send = finish(
                counts,
                source,
                terms,
                before[chunk],
                factor if step == 0 else 2.0 * factor,
                starts[chunk],
                widths[chunk],
                step < STEPS - 1,
            )
            after.append(new)
            if send:
                parts.append(to_partners(send))
        before, now = now, after
        if parts:
            products, first = left_products(parts)
    return jnp.concatenate(now, axis=2), jnp.concatenate(before, axis=2)


def solution(mesh):
    in_specs = (
        P("sec", "op", None),
        P("sec"),
        P("sec"),
        P("sec"),
        P(("sec", "op"), None, None),
        P(("sec", "op"), None, None),
    )
    out_specs = (P("sec", "op", None), P("sec", "op", None))
    step = jax.shard_map(
        functools.partial(per_device, dict(mesh.shape)),
        mesh=mesh,
        in_specs=in_specs,
        out_specs=out_specs,
        check_vma=False,
    )

    def solution(theta, *rest):
        return step(theta, *rest)

    return solution
```

```python
import functools
import math

import jax
import jax.numpy as jnp
from jax import lax
from jax.experimental import pallas as pl
from jax.experimental.pallas import tpu as pltpu
from jax.sharding import PartitionSpec as P


STEPS = 3
CORES = 2
LANES = 128
AXES = ("sec", "op")
MIB = 1 << 20

VMEM = pl.BlockSpec(memory_space=pltpu.VMEM)
SMEM = pl.BlockSpec(memory_space=pltpu.SMEM)


def params(mib):
    return pltpu.CompilerParams(vmem_limit_bytes=mib * MIB)


def partner_of(place, shift, count):
    if count & (count - 1) == 0:
        return place ^ shift
    return (place + shift) % count


def origin_of(place, shift, count):
    if count & (count - 1) == 0:
        return place ^ shift
    return (place + count - shift) % count


def split(value):
    high = value.astype(jnp.bfloat16)
    low = (value - high.astype(jnp.float32)).astype(jnp.bfloat16)
    return high, low


def widths_of(order):
    if order % (4 * LANES):
        return (order,)
    return (order // 2, order // 2)


def starts_of(widths):
    return [sum(widths[:chunk]) for chunk in range(len(widths))]


def one_dot(left_high, left_low, right_high, right_low):
    return jnp.dot(
        jnp.concatenate((left_high, left_high, left_low), axis=1),
        jnp.concatenate((right_high, right_low, right_high), axis=0),
        preferred_element_type=jnp.float32,
    )


def three_pass(left_high, left_low, right_high, right_low):
    size = left_high.shape[0] // 4
    return jnp.concatenate(
        [
            one_dot(left_high[at], left_low[at], right_high, right_low)
            for at in (slice(size * part, size * (part + 1)) for part in range(4))
        ],
        axis=0,
    )


def prepare_kernel(widths, left, right, left_high, left_low, *rights):
    left_high[0], left_low[0] = split(left[0])
    turned = right[0].T
    for chunk, (start, width) in enumerate(zip(starts_of(widths), widths)):
        part = turned[:, start : start + width]
        rights[2 * chunk][0], rights[2 * chunk + 1][0] = split(part)


def prepare(left_ops, right_ops, widths):
    pairs, order, _ = left_ops.shape

    def spec(width):
        return pl.BlockSpec((1, order, width), lambda p: (p, 0, 0))

    outs = [order] * 2 + [width for width in widths for _ in range(2)]
    high_low = pl.pallas_call(
        functools.partial(prepare_kernel, widths),
        grid=(pairs,),
        in_specs=[spec(order)] * 2,
        out_specs=[spec(width) for width in outs],
        out_shape=[
            jax.ShapeDtypeStruct((pairs, order, width), jnp.bfloat16) for width in outs
        ],
        compiler_params=params(16),
        cost_estimate=pl.CostEstimate(
            flops=4 * pairs * order * order,
            bytes_accessed=16 * pairs * order * order,
            transcendentals=0,
        ),
        name="prepare",
    )(
        pltpu.with_memory_space_constraint(left_ops, pltpu.HBM),
        pltpu.with_memory_space_constraint(right_ops, pltpu.HBM),
    )
    pairs = list(zip(high_low[::2], high_low[1::2]))
    return pairs[0], pairs[1:]


def left_kernel(count, carried, last, start, *refs):
    left_high, left_low, right_high, right_low = refs[:4]
    parts, refs = refs[4 : 4 + count], refs[4 + count :]
    before, refs = refs[:carried], refs[carried:]
    out_high, out_low = refs[:2]
    outs, (high, low, total) = refs[2:-3], refs[-3:]
    place, pair = lax.axis_index("op"), pl.program_id(0)
    rows, width = parts[0].shape

    @pl.when(pair == 0)
    def _():
        for shift in range(count):
            at = pl.ds(pl.multiple_of(origin_of(place, shift, count) * rows, rows), rows)
            high[at, :], low[at, :] = split(parts[shift][...])
        total[...] = before[0][...] if carried else jnp.zeros_like(total)

    product = three_pass(left_high[pair], left_low[pair], high[...], low[...])
    product_high, product_low = split(product)
    out_high[pair], out_low[pair] = product_high, product_low
    at = pl.ds(start, width)
    total[...] += three_pass(
        product_high, product_low, right_high[pair, at, :], right_low[pair, at, :]
    )

    @pl.when(pair == pl.num_programs(0) - 1)
    def _():
        if last:
            put_rows(total, outs, place)
        else:
            outs[0][...] = total[...]


def put_rows(total, outs, place):
    count, rows = len(outs), outs[0].shape[0]
    for shift in range(count):
        start = pl.multiple_of(partner_of(place, shift, count) * rows, rows)
        outs[shift][...] = total[pl.ds(start, rows), :]


def left_product(left, right, parts, before, start, last):
    pairs, order, _ = left[0].shape
    count = len(parts)
    rows, width = parts[0].shape
    first = right[0].shape[2]

    def whole(rows, width):
        return pl.BlockSpec((rows, width), lambda p: (0, 0))

    out = jax.ShapeDtypeStruct((pairs, order, width), jnp.bfloat16)
    pieces, height = (count, rows) if last else (1, order)
    high, low, *sums = pl.pallas_call(
        functools.partial(left_kernel, count, len(before), last, start),
        grid=(pairs,),
        in_specs=[VMEM] * 4
        + [whole(rows, width)] * count
        + [whole(order, first)] * len(before),
        out_specs=[VMEM] * 2 + [whole(height, first)] * pieces,
        out_shape=[out] * 2
        + [jax.ShapeDtypeStruct((height, first), jnp.float32)] * pieces,
        scratch_shapes=[pltpu.VMEM((order, width), jnp.bfloat16)] * 2
        + [pltpu.VMEM((order, first), jnp.float32)],
        compiler_params=params(16),
        cost_estimate=pl.CostEstimate(
            flops=6 * pairs * order * width * (order + first),
            bytes_accessed=4 * pairs * order * (order + width + first),
            transcendentals=0,
        ),
        name="left_product",
    )(*left, *right, *parts, *before)
    return (high, low), sums


def right_kernel(count, chunks, right_high, right_low, *refs):
    products = refs[: 2 * chunks]
    outs = refs[2 * chunks : 2 * chunks + count]
    total = refs[2 * chunks + count]
    place = lax.axis_index("op")
    pair = pl.program_id(0)
    term, start = 0.0, 0
    for high, low in zip(products[::2], products[1::2]):
        at = pl.ds(start, high.shape[2])
        right = right_high[pair, at, :], right_low[pair, at, :]
        term = term + three_pass(high[pair], low[pair], *right)
        start += high.shape[2]

    @pl.when(pair == 0)
    def _():
        total[...] = term

    @pl.when(pair > 0)
    def _():
        total[...] += term

    @pl.when(pair == pl.num_programs(0) - 1)
    def _():
        put_rows(total, outs, place)


def right_product(right, products, count):
    pairs, order, width = right[0].shape
    rows = order // count

    out_spec = pl.BlockSpec((rows, width), lambda p: (0, 0))
    return pl.pallas_call(
        functools.partial(right_kernel, count, len(products) // 2),
        grid=(pairs,),
        in_specs=[VMEM] * (2 + len(products)),
        out_specs=[out_spec] * count,
        out_shape=[jax.ShapeDtypeStruct((rows, width), jnp.float32)] * count,
        scratch_shapes=[pltpu.VMEM((order, width), jnp.float32)],
        compiler_params=params(16),
        cost_estimate=pl.CostEstimate(
            flops=6 * pairs * order * order * width,
            bytes_accessed=4 * pairs * order * (order + width),
            transcendentals=0,
        ),
        name="right_product",
    )(*right, *products)


def scatter_kernel(count, sec_local, chips, own_target, other_target, *refs):
    own, other, outs, home = (
        refs[:count],
        refs[count],
        refs[count + 1 : count + chips],
        refs[count + chips],
    )
    sec, place = lax.axis_index("sec"), lax.axis_index("op")
    chip, core = lax.div(sec, CORES), lax.rem(sec, CORES)
    sign = 1 - 2 * core
    for out in (*outs, home):
        out[...] = jnp.zeros_like(out)
    for shift in range(count):
        block = origin_of(place, shift, count)
        for target, part in (
            (own_target[block], own[shift]),
            (other_target[block], other.at[shift]),
        ):
            target_sec = lax.div(target, sec_local)
            target_chip = lax.div(target_sec, CORES)
            slot = lax.rem(target, CORES * sec_local)
            distance = (target_chip - chip) * sign
            for step in range(1, chips):

                @pl.when(distance == step)
                def _(part=part, slot=slot, out=outs[step - 1]):
                    out[slot] += part[...]

            @pl.when(target_sec == sec)
            def _(part=part, target=target):
                home[lax.rem(target, sec_local)] += part[...]


def scatter(own_target, other_target, own, other, sec_local, chips):
    rows, width = own[0].shape
    count = len(own)
    far = jax.ShapeDtypeStruct((CORES * sec_local, rows, width), jnp.float32)
    home = jax.ShapeDtypeStruct((sec_local, rows, width), jnp.float32)
    *outs, home = pl.pallas_call(
        functools.partial(scatter_kernel, count, sec_local, chips),
        in_specs=[SMEM] * 2 + [VMEM] * (count + 1),
        out_specs=[VMEM] * chips,
        out_shape=[far] * (chips - 1) + [home],
        compiler_params=params(16),
        cost_estimate=pl.CostEstimate(
            flops=2 * count * rows * width,
            bytes_accessed=4 * rows * width * (4 * count + 4 * chips),
            transcendentals=0,
        ),
        name="scatter",
    )(own_target, other_target, *own, other)
    return outs, home


def level_of(chips):
    sec = lax.axis_index("sec")
    chip, core = lax.div(sec, CORES), lax.rem(sec, CORES)
    return jnp.where(core == 0, chip, chips - 1 - chip)


def merge_kernel(chips, near, *refs):
    relayed, same, cross = refs[:-2], refs[-2], refs[-1]
    core = lax.rem(lax.axis_index("sec"), CORES)
    sec_local = same.shape[0]
    relays = level_of(chips) == 1 if relayed else None
    for out, owner in ((same, core), (cross, 1 - core)):
        for sector in range(sec_local):
            at = owner * sec_local + sector
            value = near[at]
            for part in relayed:
                value = value + jnp.where(relays, part[at], 0.0)
            out[sector] = value


def merge(near, relayed, chips):
    sectors, rows, width = near.shape
    half = jax.ShapeDtypeStruct((sectors // CORES, rows, width), jnp.float32)
    return pl.pallas_call(
        functools.partial(merge_kernel, chips),
        in_specs=[VMEM] * (1 + len(relayed)),
        out_specs=[VMEM] * 2,
        out_shape=[half] * 2,
        compiler_params=params(16),
        cost_estimate=pl.CostEstimate(
            flops=near.size, bytes_accessed=12 * near.size, transcendentals=0
        ),
        name="merge",
    )(near, *relayed)


def gather_kernel(chips, home, *refs):
    arrived, send, keep = refs[:-2], refs[-2], refs[-1]
    core = lax.rem(lax.axis_index("sec"), CORES)
    relays = level_of(chips) == 1
    sec_local = home.shape[0]
    for sector in range(sec_local):
        mine = core * sec_local + sector
        theirs = (1 - core) * sec_local + sector
        first = jnp.where(relays, 0.0, arrived[0][theirs])
        second = jnp.where(relays, 0.0, arrived[0][mine])
        for part in arrived[1:]:
            first, second = first + part[theirs], second + part[mine]
        send[sector], keep[sector] = first, home[sector] + second


def gather(home, arrived, chips):
    shape = jax.ShapeDtypeStruct(home.shape, jnp.float32)
    return pl.pallas_call(
        functools.partial(gather_kernel, chips),
        in_specs=[VMEM] * (1 + len(arrived)),
        out_specs=[VMEM] * 2,
        out_shape=[shape] * 2,
        compiler_params=params(16),
        cost_estimate=pl.CostEstimate(
            flops=home.size * 2 * len(arrived),
            bytes_accessed=home.size * 4 * (2 * len(arrived) + 3),
            transcendentals=0,
        ),
        name="gather",
    )(home, *arrived)


def finish_kernel(terms, olds, parts, scale, start, counts, source, *refs):
    summands, before = refs[:terms], refs[terms : terms + olds]
    new = refs[len(refs) - 1 - parts]
    outs = refs[len(refs) - parts :]
    place = lax.axis_index("op")
    sec_local, rows, width = new.shape
    row = place * rows + lax.broadcasted_iota(jnp.int32, (rows, width), 0)
    column = start + lax.broadcasted_iota(jnp.int32, (rows, width), 1)
    for sector in range(sec_local):
        value = summands[0][sector]
        for summand in summands[1:]:
            value = value + summand[sector]
        live = (row < counts[sector]) & (column < counts[sector])
        value = jnp.where(live, scale * value, 0.0)
        for part in before:
            value = value - part[sector]
        new[sector] = value
    for shift in range(parts):
        outs[shift][...] = new[source[partner_of(place, shift, parts)]]


def finish(counts, source, summands, before, into, scale, order, start, width, send):
    sec_local, rows, _ = summands[0].shape
    olds = [] if before is None else [before]
    intos = [] if into is None else [into]
    parts = source.shape[0] if send else 0

    def columns(operand):
        place = start // width if operand.shape[2] == order else 0
        return pl.BlockSpec((sec_local, rows, width), lambda i: (0, 0, place))

    new = jax.ShapeDtypeStruct((sec_local, rows, order), jnp.float32)
    part = jax.ShapeDtypeStruct((rows, width), jnp.float32)
    operands = (counts, source, *summands, *olds, *intos)
    return pl.pallas_call(
        functools.partial(
            finish_kernel, len(summands), len(olds), parts, scale, start
        ),
        grid=(1,),
        in_specs=[SMEM] * 2
        + [columns(operand) for operand in (*summands, *olds)]
        + [pl.BlockSpec(memory_space=pl.ANY)] * len(intos),
        out_specs=[columns(new)]
        + [pl.BlockSpec((rows, width), lambda i: (0, 0))] * parts,
        out_shape=[new] + [part] * parts,
        input_output_aliases={len(operands) - 1: 0} if intos else {},
        compiler_params=params(16),
        cost_estimate=pl.CostEstimate(
            flops=4 * sec_local * rows * width,
            bytes_accessed=4 * rows * width * (sec_local * 4 + parts),
            transcendentals=0,
        ),
        name="finish",
    )(*operands)


def per_device(shape, theta, counts, source, target, left_ops, right_ops):
    secs, ops = shape["sec"], shape["op"]
    chips = secs // CORES
    sec_local, _, order = theta.shape
    pairs = left_ops.shape[0]
    factor = 0.5 / math.sqrt(target.shape[0] * pairs / sec_local)

    def permute(value, where):
        pairs = []
        for sec in range(secs):
            for op in range(ops):
                to = where(sec, op)
                if to is not None:
                    pairs.append((sec * ops + op, to[0] * ops + to[1]))
        return lax.ppermute(value, AXES, pairs)

    def to_core(value):
        return permute(value, lambda sec, op: (sec ^ 1, op))

    def to_partners(parts):
        here = [parts[0]]
        for shift in range(1, ops):
            here.append(
                permute(parts[shift], lambda sec, op: (sec, partner_of(op, shift, ops)))
            )
        return here

    def along(value, steps, cross=0):
        def where(sec, op):
            chip, core = sec // CORES, sec % CORES
            level = chip if core == 0 else chips - 1 - chip
            if level not in steps or level + steps[level] >= chips:
                return None
            to = chip + (steps[level] if core == 0 else -steps[level])
            return to * CORES + (core ^ cross), op

        return permute(value, where)

    other_target = to_core(target)

    def sums(pieces):
        own = to_partners(pieces)
        other = to_core(jnp.stack(own))
        outs, home = scatter(target, other_target, own, other, sec_local, chips)
        arrived = []
        if chips > 2:
            steps = {level: 2 for level in range(1, chips)} | {0: 1}
            arrived.append(along(outs[1], steps))
        for distance in range(3, chips):
            steps = {level: distance for level in range(chips)}
            arrived.append(along(outs[distance - 1], steps))
        terms = [home]
        if arrived:
            give, keep = gather(home, arrived, chips)
            terms = [keep, to_core(give)]
        if chips > 1:
            halves = merge(outs[0], arrived[:1], chips)
            one = {level: 1 for level in range(chips)}
            for cross, half in enumerate(halves):
                terms.append(along(half, one, cross))
        return terms

    widths = widths_of(order)
    starts = starts_of(widths)
    chunks = range(len(widths))

    def next_vector(terms, before, into, scale, chunk, send):
        return finish(
            counts,
            source,
            terms,
            before,
            into,
            scale,
            order,
            starts[chunk],
            widths[chunk],
            send,
        )

    def left_products(parts):
        products, carry = [], []
        for chunk in chunks:
            product, carry = left_product(
                left,
                right[0],
                parts[chunk],
                carry,
                starts[chunk],
                chunk == chunks[-1],
            )
            products.extend(product)
        return products, carry

    before, now, parts = None, None, []
    theta = pltpu.with_memory_space_constraint(theta, pltpu.HBM)
    for chunk in chunks:
        now, *send = next_vector((theta,), None, now, 1.0, chunk, True)
        parts.append(to_partners(send))
    left, right = prepare(left_ops, right_ops, widths)
    products, first = left_products(parts)

    for step in range(STEPS):
        parts, after = [], None
        scale = factor if step == 0 else 2.0 * factor
        more = step < STEPS - 1
        for chunk in chunks:
            if chunk == 0:
                pieces = first
            else:
                pieces = right_product(right[chunk], products, ops)
            terms = sums(pieces)
            after, *send = next_vector(terms, before, after, scale, chunk, more)
            if send:
                parts.append(to_partners(send))
        before, now = now, after
        if parts:
            products, first = left_products(parts)
    return now, before


def solution(mesh):
    in_specs = (
        P("sec", "op", None),
        P("sec"),
        P("sec"),
        P("sec"),
        P(("sec", "op"), None, None),
        P(("sec", "op"), None, None),
    )
    out_specs = (P("sec", "op", None), P("sec", "op", None))
    step = jax.shard_map(
        functools.partial(per_device, dict(mesh.shape)),
        mesh=mesh,
        in_specs=in_specs,
        out_specs=out_specs,
        check_vma=False,
    )

    def solution(theta, *rest):
        return step(theta, *rest)

    return solution
```
